32 devices in a mesh: grp: 2 (over x), slc: 16 (over z, y, core).
Axes of the slice: x: 2, y: 2, z: 4, core: 2. Of those that a mesh axis runs over, the one named last changes fastest.
Arguments:
- bitstrings: int32 [1024], P('grp'), parts along dimension 0, may hold values from 0 to 511, as said below
- tree_order: int32 [12], P('grp'), parts along dimension 0, may hold values from 0 to 5, each once
- owners: int32 [12], P('grp'), parts along dimension 0, may hold values from 0 to 15
- slice_assign: int32 [64, 6], P(('grp', 'slc')), parts along dimension 0, may hold values from 0 to 63
- boundary: bfloat16 [1024, 4096], P('grp'), parts along dimension 0, may hold values from -6 to 6
- branch_pool: bfloat16 [32, 64, 4096], P(('grp', 'slc')), parts along dimension 0, may hold values from -0.75 to 0.75
- slice_tensors: bfloat16 [12, 64, 4096], P('grp'), parts along dimension 0, may hold values from -3 to 3
- closing: bfloat16 [8192, 128], P('grp'), parts along dimension 0, may hold values from -0.09375 to 0.09375
Outputs:
- amplitudes: float32 [1024, 128], P(('grp', 'slc')), parts along dimension 0
The draws below stay inside these ranges and needn't reach their ends.
There are 2 independent parts, one for each index of `grp`. The reference program is written for one: setup_inputs(seed, part) draws one part's arguments, and reference() takes and returns one part's arrays. A program takes and returns all parts, laid end to end along the dimension named above; each array names one. Nothing has to cross between parts.
Inputs may be any that keep to these rules, and one draw needn't show every extreme that they name: `bitstrings`: 512 distinct configurations. `tree_order`: a permutation of the sections.
All inputs are finite; a program needn't handle non-finite values.
Results may differ from the reference program's by a relative error of at most 0.0075.
Values may be sent and summed in bfloat16 or wider, within the bound.
A program may use at most 128 MiB of HBM per device.

```python
import math
import jax
import jax.numpy as jnp
from jax import lax

BOND = 64
PAIR = 4096
OUT = 128
NSTATES = 512
SECTIONS = 6
ROWS = 512
SLICES = 32
N_SLC = 16


def draw_bitstrings(key, part):
    key_middle = jax.random.fold_in(key, 11)
    key_order = jax.random.fold_in(key, 12)
    middle = jax.random.permutation(key_middle, NSTATES - 2)[:ROWS - 2].astype(jnp.int32) + 1
    ends = jnp.array([0, NSTATES - 1], jnp.int32)
    values = jnp.concatenate([ends, middle])
    order = jax.random.permutation(key_order, ROWS)
    return values[order].astype(jnp.int32)


def with_ends(values, rng, least, high):
    place = [jax.random.randint(jax.random.fold_in(rng, axis), (), 0, length) for axis, length in enumerate(values.shape)]
    longest = values.shape.index(max(values.shape))
    beside = place[:longest] + [(place[longest] + 1) % values.shape[longest]] + place[longest + 1:]
    return values.at[tuple(place)].set(least).at[tuple(beside)].set(high)


def level_of(key, dims, cuts, least, high):
    level = 1.0
    for position, shards_of in cuts:
        heights = jax.random.uniform(jax.random.fold_in(jax.random.fold_in(key, 6), position), (shards_of,), jnp.float32, least / len(cuts), high / len(cuts))
        level = level * jnp.repeat(jnp.exp(heights), dims[position] // shards_of).reshape((-1,) + (1,) * (len(dims) - 1 - position))
    return level


def scatter_about(rng, extent, deviation, bound, shards=(), kind=jnp.bfloat16):
    drawn = jax.random.normal(rng, extent, jnp.float32) * deviation
    if len(shards) > 0:
        drawn = level_of(rng, extent, shards, -0.22, 0.18) * drawn
    return jnp.clip(drawn, min=-bound, max=bound).astype(kind)


def setup_inputs(seed: int = 0, part: int = 0) -> dict:
    key_list = jax.random.split(jax.random.key(seed), 9)
    own_keys = jax.random.split(jax.random.fold_in(key_list[8], part), 9)
    return {
        "bitstrings": draw_bitstrings(jax.random.fold_in(jax.random.fold_in(key_list[8], part), 71), part),
        "tree_order": jax.random.permutation(own_keys[1], SECTIONS).astype(jnp.int32),
        "owners": with_ends(jax.random.randint(own_keys[2], (SECTIONS,), 0, N_SLC), jax.random.fold_in(own_keys[2], 1), 0, N_SLC - 1).astype(jnp.int32),
        "slice_assign": with_ends(jax.random.randint(own_keys[3], (SLICES, SECTIONS), 0, BOND), jax.random.fold_in(own_keys[3], 1), 0, BOND - 1).astype(jnp.int32),
        "boundary": scatter_about(own_keys[4], (NSTATES, PAIR), 1.0, 6.0),
        "branch_pool": scatter_about(own_keys[5], (N_SLC, BOND, PAIR), BOND ** -0.5, 0.75, ((0, 16),)),
        "slice_tensors": scatter_about(own_keys[6], (SECTIONS, BOND, PAIR), 1.0, 3.0),
        "closing": scatter_about(own_keys[7], (PAIR, OUT), PAIR ** -0.5, 0.09375),
    }


def reference(bitstrings, tree_order, owners, slice_assign, boundary, branch_pool, slice_tensors, closing):
    starts = jnp.take(boundary, bitstrings, axis=0)
    branches = jnp.take(branch_pool, owners, axis=0).astype(jnp.float32)

    def one_slice(assign):
        states = starts
        for section_idx in range(SECTIONS):
            product = jnp.einsum('rab,acb->rcb', states.astype(jnp.float32).reshape(ROWS, BOND, BOND), branches[section_idx].reshape(BOND, BOND, BOND))
            factor = slice_tensors[tree_order[section_idx], assign[section_idx]].astype(jnp.float32)
            states = (product.reshape(ROWS, PAIR) * factor[None, :]).astype(jnp.bfloat16)
        return jnp.dot(states, closing, preferred_element_type=jnp.float32)
    partial_amps = lax.map(one_slice, slice_assign)
    return lax.optimization_barrier(jnp.sum(partial_amps, axis=0)) * (1.0 / math.sqrt(SLICES))
```

```python
import functools
import math

import jax
import jax.numpy as jnp
from jax import lax
from jax.experimental import pallas as pl
from jax.experimental.pallas import tpu as pltpu
from jax.sharding import PartitionSpec as P

F32 = jnp.float32
BF16 = jnp.bfloat16
TILE = 16


def iota(shape, dim):
    return lax.broadcasted_iota(jnp.int32, shape, dim)


def log2(value):
    assert value & (value - 1) == 0
    return value.bit_length() - 1


def one_hot(mask):
    return jnp.where(mask, 1.0, 0.0).astype(BF16)


def dot(x, y):
    return jnp.dot(x, y, preferred_element_type=F32)


def dot_t(x, y):
    return lax.dot_general(x, y, (((1,), (1,)), ((), ())), preferred_element_type=F32)


def split(x):
    high = x.astype(BF16)
    return high, (x - high.astype(F32)).astype(BF16)


def kernel(
    n, owners, tree, assign, bits, pool_hbm, tensors_hbm, boundary_hbm, closing_hbm, out,
    pool, tensors, boundary, closing, packed, got, pick, tables, starts, close,
    factors, states, partial, terms, load_sem, send_sem, recv_sem, send2_sem, recv2_sem,
):
    me = lax.axis_index("slc")
    bond, pair = pool.shape[1], pool.shape[2]
    share = bond // n
    width = bond * share
    half = width // 2
    sections, slices = tree.shape[0], assign.shape[0]
    notes = got.shape[1] - half
    rows = partial.shape[0]
    out_rows = rows // n
    span = bond * TILE // share
    chunks = pair // span

    loads = [
        pltpu.make_async_copy(source, target, load_sem.at[i])
        for i, (source, target) in enumerate(
            ((pool_hbm, pool), (tensors_hbm, tensors), (boundary_hbm, boundary), (closing_hbm, closing))
        )
    ]
    for load in loads:
        load.start()

    barrier = pltpu.get_barrier_semaphore()

    def greet(d, carry):
        pl.semaphore_signal(
            barrier, inc=1, device_id={"slc": lax.rem(me + d, n)}, device_id_type=pl.DeviceIdType.MESH
        )
        return carry

    lax.fori_loop(1, n, greet, 0)

    r, l = iota((span, span), 0), iota((span, span), 1)
    within = jnp.bitwise_and(r, TILE - 1)
    source = (
        jnp.right_shift(within, log2(share)) * bond
        + jnp.right_shift(r, log2(TILE)) * share
        + jnp.bitwise_and(r, share - 1)
    )
    order = one_hot(source == l)
    order = jnp.concatenate([order, order], axis=1)
    blank = jnp.zeros((bond, span), BF16)
    loads[0].wait()
    for i in range(chunks // 2):
        low = pool[0, :, i * span:(i + 1) * span]
        high = pool[0, :, pair // 2 + i * span:pair // 2 + (i + 1) * span]
        both = jnp.concatenate(
            [jnp.concatenate([low, blank], axis=0), jnp.concatenate([blank, high], axis=0)], axis=1
        )
        moved = dot_t(order, both).astype(BF16)
        for j in range(n):
            packed[j, i * TILE:(i + 1) * TILE, :] = moved[j * TILE:(j + 1) * TILE, :]
    note_row = iota((notes, 2 * bond), 0)
    note = jnp.zeros((notes, 2 * bond), F32)
    for k in range(sections):
        for s in range(slices):
            note = jnp.where(note_row == k * slices + s, assign[s, k].astype(F32), note)
    note = note.astype(BF16)
    for j in range(n):
        packed[j, half:, :] = note
    got[me] = packed[me]

    pl.semaphore_wait(barrier, n - 1)

    def exchange(d):
        peer = lax.rem(me + d, n)
        return pltpu.make_async_remote_copy(
            src_ref=packed.at[peer],
            dst_ref=got.at[me],
            send_sem=send_sem.at[d],
            recv_sem=recv_sem.at[d],
            device_id={"slc": peer},
            device_id_type=pl.DeviceIdType.MESH,
        )

    def start(d, carry):
        exchange(d).start()
        return carry

    lax.fori_loop(1, n, start, 0)

    lane = iota((span, width), 1)
    wanted = (
        jnp.right_shift(lane, log2(share)) * bond + me * share + jnp.bitwise_and(lane, share - 1)
    )
    for i in range(chunks):
        pick[i * span:(i + 1) * span, :] = one_hot(iota((span, width), 0) + i * span == wanted)
    loads[1].wait()
    for k in range(sections):
        tables[k] = dot(tensors[k], pick[...]).astype(BF16)
    bits_row = bits[...].astype(F32)
    eye = iota((rows, rows), 0) == iota((rows, rows), 1)
    bits_col = jnp.sum(jnp.where(eye, bits_row, 0.0), axis=1, keepdims=True)
    states_of = one_hot(bits_col == iota((rows, boundary.shape[0]), 1).astype(F32))
    loads[2].wait()
    taken = dot(boundary[...], pick[...]).astype(BF16)
    starts[...] = dot(states_of, taken).astype(BF16)
    r, l = iota((TILE, span), 0), iota((TILE, span), 1)
    keep = one_hot(
        l == jnp.right_shift(r, log2(share)) * bond + me * share + jnp.bitwise_and(r, share - 1)
    )
    loads[3].wait()
    for i in range(chunks):
        close[i * TILE:(i + 1) * TILE, :] = dot(keep, closing[i * span:(i + 1) * span, :]).astype(BF16)

    lane_b = jnp.bitwise_and(iota((width, width), 1), share - 1)
    same_b = jnp.bitwise_and(iota((width, width), 0), share - 1) == lane_b
    r, l = iota((2 * bond, width), 0), jnp.right_shift(iota((2 * bond, width), 1), log2(share))
    widen_low, widen_high = one_hot(r == l), one_hot(r == l + bond)
    r, l = iota((bond, 2 * bond), 0), iota((bond, 2 * bond), 1)
    turn_low, turn_high = one_hot(r == l), one_hot(r + bond == l)

    def finish(d, carry):
        exchange(d).wait()
        return carry

    lax.fori_loop(1, n, finish, 0)

    values = got[:, half:, :].reshape(n * notes, 2 * bond).astype(F32)
    chosen = one_hot(values == iota((n * notes, 2 * bond), 1).astype(F32))[:, :bond]
    for k in range(sections):
        factors[k] = dot(chosen, tables[tree[k]])

    group = min(n, 8)
    block = got[owners[0]][:half]
    first = jnp.concatenate([dot_t(turn_low, block), dot_t(turn_high, block)], axis=1)

    def factor_of(k, g, i, s):
        line = factors[k, pl.ds(pl.multiple_of((g * group + i) * notes, notes), notes), :]
        return line[k * slices + s:k * slices + s + 1, :]

    step_rows = group * slices * bond
    for g in range(n // group):
        for i in range(group):
            for s in range(slices):
                at = g * step_rows + (i * slices + s) * bond
                states[at:at + bond, :] = (first * factor_of(0, g, i, s)).astype(BF16)

    total = jnp.zeros((bond, width), F32)
    for k in range(1, sections):
        block = got[owners[k]][:half]
        spread = jnp.concatenate([dot(block, widen_low), dot(block, widen_high)], axis=0)
        branch = jnp.where(same_b, spread, 0.0).astype(BF16)

        def advance(g, sofar, k=k, branch=branch):
            base = pl.multiple_of(g * step_rows, step_rows)
            product = dot_t(states[pl.ds(base, step_rows), :], branch)
            for i in range(group):
                for s in range(slices):
                    at = (i * slices + s) * bond
                    scaled = product[at:at + bond, :] * factor_of(k, g, i, s)
                    if k < sections - 1:
                        states[pl.ds(pl.multiple_of(base + at, bond), bond), :] = scaled.astype(BF16)
                    else:
                        sofar = sofar + scaled
            return sofar

        total = lax.fori_loop(0, n // group, advance, total)

    r, l = iota((width, bond), 0), iota((width, bond), 1)
    repeat = one_hot(jnp.right_shift(r, log2(share)) == l)
    weights = jnp.zeros((width, close.shape[1]), F32)
    for piece in split(total):
        wide = jnp.where(same_b, dot(repeat, piece), 0.0).astype(BF16)
        weights = weights + dot(wide, close[...])
    high, low = split(weights)
    partial[...] = dot(starts[...], high) + dot(starts[...], low)
    terms[me] = partial[pl.ds(pl.multiple_of(me * out_rows, out_rows), out_rows), :]

    def gather(d):
        peer = lax.rem(me + d, n)
        return pltpu.make_async_remote_copy(
            src_ref=partial.at[pl.ds(pl.multiple_of(peer * out_rows, out_rows), out_rows), :],
            dst_ref=terms.at[me],
            send_sem=send2_sem.at[d],
            recv_sem=recv2_sem.at[d],
            device_id={"slc": peer},
            device_id_type=pl.DeviceIdType.MESH,
        )

    def start2(d, carry):
        gather(d).start()
        return carry

    lax.fori_loop(1, n, start2, 0)

    def finish2(d, carry):
        gather(d).wait()
        return carry

    lax.fori_loop(1, n, finish2, 0)
    out[...] = jnp.sum(terms[...], axis=0) * (1.0 / math.sqrt(slices * n))


def local(
    n, bitstrings, tree_order, owners, slice_assign, boundary, branch_pool, slice_tensors, closing
):
    slices, sections = slice_assign.shape
    bond, pair = branch_pool.shape[1:]
    rows, outs = bitstrings.shape[0], closing.shape[1]
    share = bond // n
    width = bond * share
    notes = -(-slices * sections // TILE) * TILE
    smem = pl.BlockSpec(memory_space=pltpu.SMEM)
    vmem = pl.BlockSpec(memory_space=pltpu.VMEM)
    anywhere = pl.BlockSpec(memory_space=pl.ANY)
    return pl.pallas_call(
        functools.partial(kernel, n),
        out_shape=jax.ShapeDtypeStruct((rows // n, outs), F32),
        in_specs=[smem, smem, smem, vmem, anywhere, anywhere, anywhere, anywhere],
        out_specs=vmem,
        scratch_shapes=[
            pltpu.VMEM(branch_pool.shape, BF16),
            pltpu.VMEM(slice_tensors.shape, BF16),
            pltpu.VMEM(boundary.shape, BF16),
            pltpu.VMEM(closing.shape, BF16),
            pltpu.VMEM((n, width // 2 + notes, 2 * bond), BF16),
            pltpu.VMEM((n, width // 2 + notes, 2 * bond), BF16),
            pltpu.VMEM((pair, width), BF16),
            pltpu.VMEM((sections, bond, width), BF16),
            pltpu.VMEM((rows, width), BF16),
            pltpu.VMEM((width, outs), BF16),
            pltpu.VMEM((sections, n * notes, width), F32),
            pltpu.VMEM((n * slices * bond, width), BF16),
            pltpu.VMEM((rows, outs), F32),
            pltpu.VMEM((n, rows // n, outs), F32),
            pltpu.SemaphoreType.DMA((4,)),
            pltpu.SemaphoreType.DMA((n,)),
            pltpu.SemaphoreType.DMA((n,)),
            pltpu.SemaphoreType.DMA((n,)),
            pltpu.SemaphoreType.DMA((n,)),
        ],
        compiler_params=pltpu.CompilerParams(collective_id=0, has_side_effects=True),
    )(
        owners, tree_order, slice_assign, bitstrings.reshape(1, rows),
        branch_pool, slice_tensors, boundary, closing,
    )


def solution(mesh):
    return jax.shard_map(
        functools.partial(local, mesh.shape["slc"]),
        mesh=mesh,
        in_specs=(
            P("grp"),
            P("grp"),
            P("grp"),
            P(("grp", "slc"), None),
            P("grp", None),
            P(("grp", "slc"), None, None),
            P("grp", None, None),
            P("grp", None),
        ),
        out_specs=P(("grp", "slc"), None),
        check_vma=False,
    )
```
